32 devices in a mesh: row: 8 (over z, y), col: 4 (over x, core).
Axes of the slice: x: 2, y: 2, z: 4, core: 2. Of those that a mesh axis runs over, the one named last changes fastest.
Arguments:
- left_act: bfloat16 [768, 128], P(('row', 'col')), may hold values from -540 to 540
- right_act: bfloat16 [768, 128], P(('row', 'col')), may hold values from -6 to 6
- norm_gain: float32 [128], replicated, may hold values from 0.25 to 1.75
- norm_bias: float32 [128], replicated, may hold values from -3 to 3
- w_in: bfloat16 [128, 512], replicated, may hold values from -0.5 to 0.5
- b_in: float32 [512], replicated, may hold values from -3 to 3
- w_out: bfloat16 [512, 128], replicated, may hold values from -0.25 to 0.25
- w_bins: bfloat16 [128, 64], replicated, may hold values from -0.5 to 0.5
- labels: int32 [768, 768], P('row', 'col'), may hold values from 0 to 63, as said below
Outputs:
- grad_left: float32 [768, 128], P(('row', 'col'))
- grad_right: float32 [768, 128], P('col')
- grad_w_in: float32 [128, 512], replicated
- grad_w_out: float32 [512, 128], replicated
- grad_w_bins: float32 [128, 64], replicated
The draws below stay inside these ranges and needn't reach their ends.
Inputs may be any that keep to these rules, and one draw needn't show every extreme that they name: labels is symmetric: labels[i, j] equals labels[j, i].
All inputs are finite; a program needn't handle non-finite values.
Results may differ from the reference program's by a relative error of at most 0.00039.
Values may be sent and summed in bfloat16 or wider, within the bound.
A program may use at most 64 MiB of HBM per device.

```python
import jax
import jax.numpy as jnp
from jax import lax

C = 128
H = 512
BINS = 64
L = 768


def draw_left_act(key, part):
    sample = jnp.clip(jax.random.normal(key, (L, C), jnp.float32), -6.0, 6.0)
    return sample.astype(jnp.bfloat16)


def draw_labels(key, part):
    upper = jax.random.randint(key, (L, L), 0, BINS)
    places = lax.iota(jnp.int32, L)
    upper_half = places[:, None] <= places[None, :]
    return jnp.where(upper_half, upper, upper.T)


def shard_levels(stream_key, dims, shards, low, top_value):
    def one(dim, blocks):
        draws = jax.random.uniform(jax.random.fold_in(jax.random.fold_in(stream_key, 6), dim), (blocks,), jnp.float32, low / len(shards), top_value / len(shards))
        return jnp.repeat(jnp.exp(draws), dims[dim] // blocks).reshape((-1,) + (1,) * (len(dims) - dim - 1))

    factor_of = one(*shards[0])
    for cut in shards[1:]:
        factor_of = factor_of * one(*cut)
    return factor_of


def scatter_about(stream_key, dims, scale, bound, cuts=(), held_as=jnp.bfloat16):
    level = shard_levels(stream_key, dims, cuts, -0.22, 0.18) if cuts else 1.0
    entries = jax.random.normal(stream_key, dims, jnp.float32) * scale * level
    return jnp.minimum(jnp.maximum(entries, -bound), bound).astype(held_as)


def setup_inputs(seed: int = 0) -> dict:
    seeds = jax.random.split(jax.random.key(seed), 10)
    left_act = draw_left_act(jax.random.fold_in(seeds[9], 71), 0)
    right_act = scatter_about(seeds[1], (L, C), 1.0, 6.0, ((0, 32),))
    norm_gain = jnp.clip(1.0 + 0.15 * jax.random.normal(seeds[2], (C,), jnp.float32), 0.25, 1.75)
    norm_bias = scatter_about(seeds[3], (C,), 0.5, 3.0, (), jnp.float32)
    w_in = scatter_about(seeds[4], (C, H), C ** -0.5, 0.5)
    b_in = scatter_about(seeds[5], (H,), 0.5, 3.0, (), jnp.float32)
    w_out = scatter_about(seeds[6], (H, C), H ** -0.5, 0.25)
    w_bins = scatter_about(seeds[7], (C, BINS), C ** -0.5, 0.5)
    labels = draw_labels(jax.random.fold_in(seeds[9], 71), 0)
    return {"left_act": left_act, "right_act": right_act, "norm_gain": norm_gain, "norm_bias": norm_bias, "w_in": w_in, "b_in": b_in, "w_out": w_out, "w_bins": w_bins, "labels": labels}


def inner(first, second):
    return lax.dot_general(first, second, (((0,), (0,)), ((), ())), preferred_element_type=jnp.float32)

def outer(first, second):
    return lax.dot_general(first, second, (((1,), (1,)), ((), ())), preferred_element_type=jnp.float32)

def transition(left_rows, right_cols, gain, bias, w_in, b_in, w_out):
    summed = (left_rows.astype(jnp.float32)[:, None, :] + right_cols.astype(jnp.float32)[None, :, :]).reshape(-1, left_rows.shape[1])
    center = summed - lax.optimization_barrier(jnp.mean(summed, axis=-1, keepdims=True))
    inv_scale = lax.rsqrt(lax.optimization_barrier(jnp.mean(center * center, axis=-1, keepdims=True)) + 1e-05)
    normal_form = center * inv_scale
    normed = (normal_form * gain + bias).astype(jnp.bfloat16)
    pre_act = jnp.dot(normed, w_in, preferred_element_type=jnp.float32) + b_in
    hidden = (pre_act * jax.nn.sigmoid(pre_act)).astype(jnp.bfloat16)
    updated = (summed + jnp.dot(hidden, w_out, preferred_element_type=jnp.float32)).astype(jnp.bfloat16)
    return (normal_form, inv_scale, normed, pre_act, hidden, updated)

def pair_backward(sym, bin_labels, parts, gain, w_in, w_out, w_bins):
    normal_form, inv_scale, normed, pre_act, hidden, updated = parts
    shifted = sym - lax.optimization_barrier(jnp.max(sym, axis=-1, keepdims=True))
    expo = jnp.exp(shifted)
    probs = expo / lax.optimization_barrier(jnp.sum(expo, axis=-1, keepdims=True))
    onehot = (bin_labels[..., None] == lax.iota(jnp.int32, sym.shape[-1])).astype(jnp.float32)
    logit_grad = (2.0 * (probs - onehot)).reshape(-1, sym.shape[-1]).astype(jnp.bfloat16)
    grad_bins = inner(updated, logit_grad)
    upd_grad = outer(logit_grad, w_bins)
    upd_half = upd_grad.astype(jnp.bfloat16)
    grad_out = inner(hidden, upd_half)
    hid_grad = outer(upd_half, w_out)
    sigma = jax.nn.sigmoid(pre_act)
    pre_grad = (hid_grad * sigma * (1.0 + pre_act * (1.0 - sigma))).astype(jnp.bfloat16)
    grad_in = inner(normed, pre_grad)
    norm_grad = outer(pre_grad, w_in) * gain
    pair_grad = inv_scale * (norm_grad - lax.optimization_barrier(jnp.mean(norm_grad, axis=-1, keepdims=True)) - normal_form * lax.optimization_barrier(jnp.mean(norm_grad * normal_form, axis=-1, keepdims=True))) + upd_grad
    return (grad_in, grad_out, grad_bins, pair_grad)

def reference(left_act, right_act, norm_gain, norm_bias, w_in, b_in, w_out, w_bins, labels):
    residues, width = left_act.shape
    stride_rows = 8
    groups = residues // stride_rows
    left_groups = left_act.reshape(groups, stride_rows, width)
    right_groups = right_act.reshape(groups, stride_rows, width)

    def forward(record):
        parts = transition(record[0], right_act, norm_gain, norm_bias, w_in, b_in, w_out)
        return jnp.dot(parts[5], w_bins, preferred_element_type=jnp.float32).reshape(stride_rows, residues, -1)
    logits = lax.map(forward, (left_groups, right_groups)).reshape(residues, residues, -1)

    def advance(running, record):
        position, left_rows, bin_labels = record
        own = lax.dynamic_slice_in_dim(logits, position * stride_rows, stride_rows, 0)
        far = jnp.transpose(lax.dynamic_slice_in_dim(logits, position * stride_rows, stride_rows, 1), (1, 0, 2))
        parts = transition(left_rows, right_act, norm_gain, norm_bias, w_in, b_in, w_out)
        grads = pair_backward(own + far, bin_labels, parts, norm_gain, w_in, w_out, w_bins)
        pair_grad = grads[3].reshape(stride_rows, residues, width)
        running = (running[0] + grads[0], running[1] + grads[1], running[2] + grads[2], running[3] + lax.optimization_barrier(jnp.sum(pair_grad, axis=0)))
        return (running, lax.optimization_barrier(jnp.sum(pair_grad, axis=1)))
    start = (jnp.zeros((width, w_in.shape[1]), jnp.float32), jnp.zeros((w_in.shape[1], width), jnp.float32), jnp.zeros((width, w_bins.shape[1]), jnp.float32), jnp.zeros((residues, width), jnp.float32))
    positions = jnp.arange(groups, dtype=jnp.int32)
    running, left_terms = lax.scan(advance, start, (positions, left_groups, labels.reshape(groups, stride_rows, residues)))
    grad_left = left_terms.reshape(residues, width)
    return (grad_left, running[3], running[0] / residues, running[1] / residues, running[2] / residues)
```

```python
import jax
import jax.numpy as jnp
import numpy as np
from jax import lax
from jax.experimental import pallas as pl
from jax.experimental.pallas import tpu as pltpu
from jax.sharding import PartitionSpec as P

UNITS = 6
SUB = 8
F32 = jnp.float32
BF16 = jnp.bfloat16


def dims(first, second):
    return (((first,), (second,)), ((), ()))


def schedule(rows, cols, tile_rows, tile_cols):
    plans = []
    for r in range(rows):
        for c in range(cols):
            plan = []
            for i in range(tile_rows // SUB):
                for j in range(tile_cols // SUB):
                    big_i = r * tile_rows // SUB + i
                    big_j = c * tile_cols // SUB + j
                    if big_i == big_j:
                        plan.append((i, j, 1))
                    elif ((big_i + big_j) % 2 == 1) == (big_j > big_i):
                        plan.append((i, j, 2))
            plans.append(plan)
    longest = -(-max(map(len, plans)) // UNITS) * UNITS
    table = np.zeros((len(plans), 3, longest + 1), np.int32)
    for place, plan in enumerate(plans):
        table[place, :, : len(plan)] = np.array(plan, np.int32).T
        table[place, 0, longest] = -(-len(plan) // UNITS)
    return table


def pair_kernel(
    tab, left_i, right_i, left_j, right_j, gain_ref, bias_ref, w_in_h, b_h, w_out_ref, w_in_t,
    w_out_t_h, bins_t2, bins_t, lab,
    g_in, g_out, g_bins, o_left_i, o_right_i, o_left_j, o_right_j,
    raw_li, raw_ri, cen_li, cen_ri, raw_lj, raw_rj, cen_lj, cen_rj, acc_li, acc_ri, acc_bins,
):
    width = gain_ref.shape[1]
    scale = 1.0 / width
    half = UNITS * SUB * SUB
    last = tab.shape[1] - 1
    col_blocks = left_j.shape[0] // SUB

    for source, raw, cen in ((left_i, raw_li, cen_li), (right_i, raw_ri, cen_ri)):
        value = source[...].astype(F32)
        mid = value - jnp.sum(value, axis=-1, keepdims=True) * scale
        raw[...] = jnp.broadcast_to(value[:, None, :], raw.shape)
        cen[...] = jnp.broadcast_to(mid[:, None, :], cen.shape)
    for source, raw, cen in ((left_j, raw_lj, cen_lj), (right_j, raw_rj, cen_rj)):
        value = source[...].astype(F32)
        raw[...] = value
        cen[...] = value - jnp.sum(value, axis=-1, keepdims=True) * scale
    for ref in (g_in, g_out, acc_bins, o_left_j, o_right_j, acc_li, acc_ri):
        ref[...] = jnp.zeros_like(ref)

    lane = lax.broadcasted_iota(jnp.int32, (1, 2 * SUB * SUB), 1)
    first_half = lane < SUB * SUB

    def step(s, carry):
        places = [(tab[0, s * UNITS + u], tab[1, s * UNITS + u]) for u in range(UNITS)]
        rows = [pl.ds(pl.multiple_of(i * SUB, SUB), SUB) for i, j in places]
        cols = [pl.ds(pl.multiple_of(j * SUB, SUB), SUB) for i, j in places]

        def grid(li, rj, ri, lj):
            own = [(li[a] + rj[b][None]).reshape(SUB * SUB, width) for a, b in zip(rows, cols)]
            far = [(ri[a] + lj[b][None]).reshape(SUB * SUB, width) for a, b in zip(rows, cols)]
            return jnp.concatenate(own + far, axis=0)

        center = grid(cen_li, cen_rj, cen_ri, cen_lj)
        inv = lax.rsqrt(jnp.sum(center * center, axis=-1, keepdims=True) * scale + 1e-05)
        form = center * inv
        normed = (form * gain_ref[...] + bias_ref[...]).astype(BF16)
        u = jnp.dot(normed, w_in_h[...], preferred_element_type=F32) + b_h[...]
        t = jnp.tanh(u)
        up = 1.0 + t
        act = u * up
        slope = up + act * (1.0 - t)
        hidden = act.astype(BF16)
        updated = (
            grid(raw_li, raw_rj, raw_ri, raw_lj)
            + jnp.dot(hidden, w_out_ref[...], preferred_element_type=F32)
        ).astype(BF16)
        both = jnp.concatenate([updated[:half], updated[half:]], axis=1)
        sym = lax.dot_general(bins_t2[...], both, dims(1, 1), preferred_element_type=F32)
        expo = jnp.exp(sym - jnp.max(sym, axis=0, keepdims=True))
        probs = expo / jnp.sum(expo, axis=0, keepdims=True)
        labs, scales = [], []
        for u0 in range(0, UNITS, 2):
            (ia, ja), (ib, jb) = places[u0], places[u0 + 1]
            labs.append(
                jnp.where(first_half, lab[ia * col_blocks + ja], lab[ib * col_blocks + jb])
            )
            wa = tab[2, s * UNITS + u0].astype(F32)
            wb = tab[2, s * UNITS + u0 + 1].astype(F32)
            scales.append(jnp.where(first_half, wa, wb))
        labs = jnp.concatenate(labs, axis=1)
        scales = jnp.concatenate(scales, axis=1)
        hit = lax.broadcasted_iota(jnp.int32, sym.shape, 0) == labs
        logit_grad = ((probs - jnp.where(hit, 1.0, 0.0)) * scales).astype(BF16)
        acc_bins[...] += jnp.dot(logit_grad, both, preferred_element_type=F32)
        upd_grad = lax.dot_general(
            logit_grad, bins_t[...], dims(0, 0), preferred_element_type=F32
        )
        upd_half = upd_grad.astype(BF16)
        hid_grad = jnp.dot(upd_half, w_out_t_h[...], preferred_element_type=F32)
        pre_grad = jnp.concatenate(
            [(hid_grad * slope[:half]).astype(BF16), (hid_grad * slope[half:]).astype(BF16)], axis=0
        )
        g_in[...] += lax.dot_general(normed, pre_grad, dims(0, 0), preferred_element_type=F32)
        g_out[...] += lax.dot_general(
            jnp.concatenate([upd_half, upd_half], axis=0), hidden, dims(0, 0),
            preferred_element_type=F32,
        )
        norm_grad = jnp.dot(pre_grad, w_in_t[...], preferred_element_type=F32) * gain_ref[...]
        mean = jnp.sum(norm_grad, axis=-1, keepdims=True) * scale
        mixed = jnp.sum(norm_grad * form, axis=-1, keepdims=True) * scale
        pair = inv * (norm_grad - mean - form * mixed)
        own = (pair[:half] + upd_grad).reshape(UNITS, SUB, SUB, width)
        far = (pair[half:] + upd_grad).reshape(UNITS, SUB, SUB, width)
        for k in range(UNITS):
            acc_li[rows[k]] += own[k]
            o_right_j[cols[k]] += jnp.sum(own[k], axis=0)
            acc_ri[rows[k]] += far[k]
            o_left_j[cols[k]] += jnp.sum(far[k], axis=0)
        return carry

    lax.fori_loop(0, tab[0, last], step, 0)
    o_left_i[...] = jnp.sum(acc_li[...], axis=1)
    o_right_i[...] = jnp.sum(acc_ri[...], axis=1)
    g_bins[...] = acc_bins[:, :width] + acc_bins[:, width:]


def pair_work(tab, left_i, right_i, left_j, right_j, gain, bias, w_in, b_in, w_out, w_bins, labels):
    tile_rows, tile_cols = labels.shape
    width, hidden = w_in.shape
    bins = w_bins.shape[1]
    blocks = labels.reshape(tile_rows // SUB, SUB, tile_cols // SUB, SUB)
    blocks = jnp.transpose(blocks, (0, 2, 1, 3)).reshape(-1, 1, SUB * SUB)
    lab = jnp.concatenate([blocks, blocks], axis=2)
    bins_t = w_bins.T
    half = jnp.asarray(0.5, BF16)
    vmem = pl.BlockSpec(memory_space=pltpu.VMEM)
    shape = jax.ShapeDtypeStruct
    return pl.pallas_call(
        pair_kernel,
        out_shape=(
            shape((width, hidden), F32), shape((width, hidden), F32), shape((bins, width), F32),
            shape((tile_rows, width), F32), shape((tile_rows, width), F32),
            shape((tile_cols, width), F32), shape((tile_cols, width), F32),
        ),
        in_specs=[pl.BlockSpec(memory_space=pltpu.SMEM)] + [vmem] * 14,
        out_specs=(vmem,) * 7,
        scratch_shapes=[pltpu.VMEM((tile_rows, SUB, width), F32)] * 4
        + [pltpu.VMEM((tile_cols, width), F32)] * 4
        + [pltpu.VMEM((tile_rows, SUB, width), F32)] * 2
        + [pltpu.VMEM((bins, 2 * width), F32)],
    )(
        tab, left_i, right_i, left_j, right_j, gain[None], bias[None], w_in * half,
        (b_in * 0.5)[None], w_out, w_in.T, w_out.T * half,
        jnp.concatenate([bins_t, bins_t], axis=1), bins_t, lab,
    )


def on_device(plans, left_act, right_act, norm_gain, norm_bias, w_in, b_in, w_out, w_bins, labels):
    tile_rows, tile_cols = labels.shape
    width = left_act.shape[1]
    row, col = lax.axis_index("row"), lax.axis_index("col")
    stacked = jnp.stack([left_act, right_act])
    everything = lax.all_gather(stacked, ("row", "col"), axis=1, tiled=True)
    residues = everything.shape[1]
    mine = lax.dynamic_slice_in_dim(everything, row * tile_rows, tile_rows, 1)
    theirs = lax.dynamic_slice_in_dim(everything, col * tile_cols, tile_cols, 1)
    tab = lax.dynamic_index_in_dim(plans, row * lax.axis_size("col") + col, 0, keepdims=False)
    g_in, g_out, g_bins, left_i, right_i, left_j, right_j = pair_work(
        tab, mine[0], mine[1], theirs[0], theirs[1], norm_gain, norm_bias, w_in, b_in, w_out,
        w_bins, labels,
    )
    whole = jnp.zeros((2, residues, width), F32)
    by_row = lax.dynamic_update_slice(whole, jnp.stack([left_i, right_i]), (0, row * tile_rows, 0))
    by_col = lax.dynamic_update_slice(whole, jnp.stack([left_j, right_j]), (0, col * tile_cols, 0))
    packed = jnp.concatenate(
        [(by_row + by_col).reshape(-1, width), g_in.reshape(-1, width), g_out.reshape(-1, width),
         g_bins.reshape(-1, width)], axis=0
    )
    total = lax.psum(packed, ("row", "col"))
    own = left_act.shape[0]
    grad_left = lax.dynamic_slice_in_dim(total, (row * lax.axis_size("col") + col) * own, own, 0)
    grad_right = lax.dynamic_slice_in_dim(total, residues + col * tile_cols, tile_cols, 0)
    rest = total[2 * residues :] / residues
    first, second = g_in.size // width, g_out.size // width
    return (
        grad_left,
        grad_right,
        rest[:first].reshape(g_in.shape),
        rest[first : first + second].reshape(g_out.shape).T,
        rest[first + second :].reshape(g_bins.shape).T,
    )


def solution(mesh):
    placed = (
        P(("row", "col"), None),
        P(("row", "col"), None),
        P(),
        P(),
        P(),
        P(),
        P(),
        P(),
        P("row", "col"),
    )
    rows, cols = mesh.shape["row"], mesh.shape["col"]

    def step(*args):
        residues = args[8].shape[0]
        plans = jnp.asarray(schedule(rows, cols, residues // rows, residues // cols))
        return jax.shard_map(
            lambda *local: on_device(plans, *local),
            mesh=mesh,
            in_specs=placed,
            out_specs=(P(("row", "col"), None), P("col", None), P(), P(), P()),
            check_vma=False,
        )(*args)

    return step
```

```python
import functools

import jax
import jax.numpy as jnp
import numpy as np
from jax import lax
from jax.experimental import pallas as pl
from jax.experimental.pallas import tpu as pltpu
from jax.sharding import PartitionSpec as P

UNITS = 6
SUB = 8
F32 = jnp.float32
BF16 = jnp.bfloat16


def dims(first, second):
    return (((first,), (second,)), ((), ()))


def schedule(rows, cols, tile_rows, tile_cols):
    plans = []
    for r in range(rows):
        for c in range(cols):
            plan = []
            for i in range(tile_rows // SUB):
                for j in range(tile_cols // SUB):
                    big_i = r * tile_rows // SUB + i
                    big_j = c * tile_cols // SUB + j
                    if big_i == big_j:
                        plan.append((i, j, 1))
                    elif ((big_i + big_j) % 2 == 1) == (big_j > big_i):
                        plan.append((i, j, 2))
            plans.append(plan)
    longest = -(-max(map(len, plans)) // UNITS) * UNITS
    table = np.zeros((len(plans), 3, longest + 1), np.int32)
    for place, plan in enumerate(plans):
        table[place, :, : len(plan)] = np.array(plan, np.int32).T
        table[place, 0, longest] = -(-len(plan) // UNITS)
    return table


def pair_kernel(
    tab, row_in, col_in, gain_ref, bias_ref, w_in_ref, b_ref, w_out_ref, w_bins_ref, lab,
    packed, res_i, res_j,
    w_in_h, b_h, w_in_t, w_out_t_h, bins_t2, bins_t, raw_li, raw_ri, cen_li, cen_ri, raw_lj,
    raw_rj, cen_lj, cen_rj, acc_li, acc_ri, o_left_j, o_right_j, g_in, g_out, acc_bins,
):
    width = gain_ref.shape[1]
    scale = 1.0 / width
    half = UNITS * SUB * SUB
    last = tab.shape[1] - 1
    col_blocks = raw_lj.shape[0] // SUB

    chunk = row_in.shape[2]

    def whole(source, side):
        parts = [source[k, side].astype(F32) for k in range(source.shape[0])]
        return jnp.concatenate(parts, axis=0)

    for side, raw, cen in ((0, raw_li, cen_li), (1, raw_ri, cen_ri)):
        value = whole(row_in, side)
        mid = value - jnp.sum(value, axis=-1, keepdims=True) * scale
        raw[...] = jnp.broadcast_to(value[:, None, :], raw.shape)
        cen[...] = jnp.broadcast_to(mid[:, None, :], cen.shape)
    for side, raw, cen in ((0, raw_lj, cen_lj), (1, raw_rj, cen_rj)):
        value = whole(col_in, side)
        raw[...] = value
        cen[...] = value - jnp.sum(value, axis=-1, keepdims=True) * scale
    w_in = w_in_ref[...].astype(F32)
    w_in_h[...] = (w_in * 0.5).astype(BF16)
    w_in_t[...] = w_in.T.astype(BF16)
    b_h[...] = b_ref[...] * 0.5
    w_out_t_h[...] = (w_out_ref[...].astype(F32) * 0.5).T.astype(BF16)
    turned = w_bins_ref[...].astype(F32).T.astype(BF16)
    bins_t[...] = turned
    bins_t2[...] = jnp.concatenate([turned, turned], axis=1)
    for ref in (g_in, g_out, acc_bins, o_left_j, o_right_j, acc_li, acc_ri):
        ref[...] = jnp.zeros_like(ref)

    lane = lax.broadcasted_iota(jnp.int32, (1, 2 * SUB * SUB), 1)
    first_half = lane < SUB * SUB

    def step(s, carry):
        places = [(tab[0, s * UNITS + u], tab[1, s * UNITS + u]) for u in range(UNITS)]
        rows = [pl.ds(pl.multiple_of(i * SUB, SUB), SUB) for i, j in places]
        cols = [pl.ds(pl.multiple_of(j * SUB, SUB), SUB) for i, j in places]

        def grid(li, rj, ri, lj):
            own = [(li[a] + rj[b][None]).reshape(SUB * SUB, width) for a, b in zip(rows, cols)]
            far = [(ri[a] + lj[b][None]).reshape(SUB * SUB, width) for a, b in zip(rows, cols)]
            return jnp.concatenate(own + far, axis=0)

        center = grid(cen_li, cen_rj, cen_ri, cen_lj)
        inv = lax.rsqrt(jnp.sum(center * center, axis=-1, keepdims=True) * scale + 1e-05)
        form = center * inv
        normed = (form * gain_ref[...] + bias_ref[...]).astype(BF16)
        u = jnp.dot(normed, w_in_h[...], preferred_element_type=F32) + b_h[...]
        t = jnp.tanh(u)
        up = 1.0 + t
        act = u * up
        slope = up + act * (1.0 - t)
        hidden = act.astype(BF16)
        updated = (
            grid(raw_li, raw_rj, raw_ri, raw_lj)
            + jnp.dot(hidden, w_out_ref[...], preferred_element_type=F32)
        ).astype(BF16)
        both = jnp.concatenate([updated[:half], updated[half:]], axis=1)
        sym = lax.dot_general(bins_t2[...], both, dims(1, 1), preferred_element_type=F32)
        expo = jnp.exp(sym - jnp.max(sym, axis=0, keepdims=True))
        probs = expo / jnp.sum(expo, axis=0, keepdims=True)
        labs, scales = [], []
        for u0 in range(0, UNITS, 2):
            (ia, ja), (ib, jb) = places[u0], places[u0 + 1]
            labs.append(
                jnp.where(first_half, lab[ia * col_blocks + ja], lab[ib * col_blocks + jb])
            )
            wa = tab[2, s * UNITS + u0].astype(F32)
            wb = tab[2, s * UNITS + u0 + 1].astype(F32)
            scales.append(jnp.where(first_half, wa, wb))
        labs = jnp.concatenate(labs, axis=1)
        scales = jnp.concatenate(scales, axis=1)
        hit = lax.broadcasted_iota(jnp.int32, sym.shape, 0) == labs
        logit_grad = ((probs - jnp.where(hit, 1.0, 0.0)) * scales).astype(BF16)
        acc_bins[...] += jnp.dot(logit_grad, both, preferred_element_type=F32)
        upd_grad = lax.dot_general(
            logit_grad, bins_t[...], dims(0, 0), preferred_element_type=F32
        )
        upd_half = upd_grad.astype(BF16)
        hid_grad = jnp.dot(upd_half, w_out_t_h[...], preferred_element_type=F32)
        pre_grad = jnp.concatenate(
            [(hid_grad * slope[:half]).astype(BF16), (hid_grad * slope[half:]).astype(BF16)], axis=0
        )
        g_in[...] += lax.dot_general(normed, pre_grad, dims(0, 0), preferred_element_type=F32)
        g_out[...] += lax.dot_general(
            jnp.concatenate([upd_half, upd_half], axis=0), hidden, dims(0, 0),
            preferred_element_type=F32,
        )
        norm_grad = jnp.dot(pre_grad, w_in_t[...], preferred_element_type=F32) * gain_ref[...]
        mean = jnp.sum(norm_grad, axis=-1, keepdims=True) * scale
        mixed = jnp.sum(norm_grad * form, axis=-1, keepdims=True) * scale
        pair = inv * (norm_grad - mean - form * mixed)
        own = (pair[:half] + upd_grad).reshape(UNITS, SUB, SUB, width)
        far = (pair[half:] + upd_grad).reshape(UNITS, SUB, SUB, width)
        for k in range(UNITS):
            acc_li[rows[k]] += own[k]
            o_right_j[cols[k]] += jnp.sum(own[k], axis=0)
            acc_ri[rows[k]] += far[k]
            o_left_j[cols[k]] += jnp.sum(far[k], axis=0)
        return carry

    lax.fori_loop(0, tab[0, last], step, 0)
    for side, acc in ((0, acc_li), (1, acc_ri)):
        value = jnp.sum(acc[...], axis=1)
        for k in range(res_i.shape[0]):
            res_i[k, side] = value[k * chunk : (k + 1) * chunk]
    for side, acc in ((0, o_left_j), (1, o_right_j)):
        for k in range(res_j.shape[0]):
            res_j[k, side] = acc[k * chunk : (k + 1) * chunk]
    hidden_width = g_in.shape[1]
    for k in range(hidden_width // width):
        packed[k * width : (k + 1) * width] = g_in[:, k * width : (k + 1) * width]
    packed[hidden_width : 2 * hidden_width] = g_out[...].T
    end = 2 * hidden_width + acc_bins.shape[0]
    packed[2 * hidden_width : end] = acc_bins[:, :width] + acc_bins[:, width:]
    if end < packed.shape[0]:
        packed[end:] = jnp.zeros((packed.shape[0] - end, width), F32)


def pair_work(tab, row_in, col_in, gain, bias, w_in, b_in, w_out, w_bins, labels, packed_rows):
    tile_rows, tile_cols = labels.shape
    width, hidden = w_in.shape
    bins = w_bins.shape[1]
    blocks = labels.reshape(tile_rows // SUB, SUB, tile_cols // SUB, SUB)
    blocks = jnp.transpose(blocks, (0, 2, 1, 3)).reshape(-1, 1, SUB * SUB)
    lab = jnp.concatenate([blocks, blocks], axis=2)
    vmem = pl.BlockSpec(memory_space=pltpu.VMEM)
    shape = jax.ShapeDtypeStruct
    return pl.pallas_call(
        pair_kernel,
        out_shape=(
            shape((packed_rows, width), F32), shape(row_in.shape, F32), shape(col_in.shape, F32),
        ),
        in_specs=[pl.BlockSpec(memory_space=pltpu.SMEM)] + [vmem] * 9,
        out_specs=(vmem,) * 3,
        scratch_shapes=[
            pltpu.VMEM((width, hidden), BF16), pltpu.VMEM((1, hidden), F32),
            pltpu.VMEM((hidden, width), BF16), pltpu.VMEM((width, hidden), BF16),
            pltpu.VMEM((bins, 2 * width), BF16), pltpu.VMEM((bins, width), BF16),
        ]
        + [pltpu.VMEM((tile_rows, SUB, width), F32)] * 4
        + [pltpu.VMEM((tile_cols, width), F32)] * 4
        + [pltpu.VMEM((tile_rows, SUB, width), F32)] * 2
        + [pltpu.VMEM((tile_cols, width), F32)] * 2
        + [pltpu.VMEM((width, hidden), F32)] * 2
        + [pltpu.VMEM((bins, 2 * width), F32)],
        name="pairs",
    )(tab, row_in, col_in, gain[None], bias[None], w_in, b_in[None], w_out, w_bins, lab)


def partners(rows, cols):
    r, c = lax.axis_index("row"), lax.axis_index("col")
    place = r * cols + c
    home = place // rows
    slot = place % rows

    def owner(m):
        k = c * rows + m
        return (k // cols, k % cols)

    return r, c, home, slot, owner


def unless(skip, action):
    if skip is None:
        action()
    else:
        pl.when(jnp.logical_not(skip))(action)


def greet(rows, cols, with_column):
    r, c, home, slot, owner = partners(rows, cols)
    barrier = pltpu.get_barrier_semaphore()

    def hello(device, skip):
        unless(skip, lambda: pl.semaphore_signal(
            barrier, inc=1, device_id=device, device_id_type=pl.DeviceIdType.MESH))

    for k in range(cols):
        hello((r, k), k == c)
    for k in range(rows):
        if with_column:
            hello((k, c), k == r)
        hello((k, home), jnp.logical_and(k == r, home == c))
        hello(owner(k), jnp.logical_and(home == c, k == slot))
    count = cols - 1 + 2 * rows + (rows - 1 if with_column else 0)
    pl.semaphore_wait(barrier, count - 2 * jnp.where(home == c, 1, 0))


def remote(src, dst, send, recv, device):
    return pltpu.make_async_remote_copy(
        src_ref=src, dst_ref=dst, send_sem=send, recv_sem=recv, device_id=device,
        device_id_type=pl.DeviceIdType.MESH,
    )


def gather_kernel(rows, cols, left, right, row_out, col_out, s_row, r_row, s_col, r_col):
    r, c, home, slot, owner = partners(rows, cols)
    here = home == c
    greet(rows, cols, False)
    sides = ((0, left), (1, right))

    def row_copy(side, src, k, at):
        return remote(src, row_out.at[at, side], s_row.at[k, side], r_row.at[at, side], (r, k))

    def col_copy(side, src, k, at, device):
        return remote(src, col_out.at[at, side], s_col.at[k, side], r_col.at[at, side], device)

    for side, src in sides:
        for k in range(rows):
            unless(jnp.logical_and(here, k == r),
                   lambda: col_copy(side, src, k, slot, (k, home)).start())
        for k in range(cols):
            unless(k == c, lambda: row_copy(side, src, k, c).start())
    for side, src in sides:
        row_out[c, side] = src[...]

        @pl.when(here)
        def _():
            col_out[slot, side] = src[...]

    for side, src in sides:
        for k in range(cols):
            unless(k == c, lambda: row_copy(side, src, k, k).wait_recv())
        for k in range(rows):
            unless(jnp.logical_and(here, k == slot),
                   lambda: col_copy(side, src, k, k, owner(k)).wait_recv())
    for side, src in sides:
        for k in range(cols):
            unless(k == c, lambda: row_copy(side, src, k, c).wait_send())
        for k in range(rows):
            unless(jnp.logical_and(here, k == r),
                   lambda: col_copy(side, src, k, slot, (k, home)).wait_send())


def reduce_kernel(
    rows, cols, residues, mine, res_i, res_j, o_left, o_right, o_in, o_out, o_bins,
    got1, sum1, got2, total, got_i, got_j, right_sum,
    s1, r1, s2, r2, s3, r3, s4, r4, si, ri, sj, rj, sb, rb,
):
    r, c, home, slot, owner = partners(rows, cols)
    here = home == c
    greet(rows, cols, True)
    width = total.shape[-1]

    def one(k, at):
        return remote(mine.at[k], got1.at[at], s1.at[k], r1.at[at], (r, k))

    def two(k, at):
        return remote(sum1.at[k], got2.at[at], s2.at[k], r2.at[at], (k, c))

    def three(k, at):
        return remote(total.at[c, r], total.at[c, at], s3.at[k], r3.at[at], (k, c))

    def four(k, at):
        return remote(total.at[c], total.at[at], s4.at[k], r4.at[at], (r, k))

    def share_i(k, at):
        return remote(res_i.at[k], got_i.at[at], si.at[k], ri.at[at], (r, k))

    def share_j(k, at, device):
        return remote(res_j.at[k], got_j.at[at], sj.at[k], rj.at[at], device)

    def spread(k, at, device):
        return remote(right_sum, o_right.at[at], sb.at[k], rb.at[at], device)

    for k in range(cols):
        unless(k == c, lambda: one(k, c).start())
    for k in range(cols):
        unless(k == c, lambda: share_i(k, c).start())
    for k in range(rows):
        unless(jnp.logical_and(here, k == slot), lambda: share_j(k, r, owner(k)).start())
    got1[c] = mine[c]
    got_i[c] = res_i[c]

    @pl.when(here)
    def _():
        got_j[r] = res_j[slot]

    for k in range(cols):
        unless(k == c, lambda: one(k, k).wait_recv())
    acc = got1[0]
    for k in range(1, cols):
        acc = acc + got1[k]
    sum1[...] = acc
    for k in range(rows):
        unless(k == r, lambda: two(k, r).start())
    got2[r] = sum1[r]
    for k in range(cols):
        unless(k == c, lambda: share_i(k, k).wait_recv())
    for k in range(rows):
        unless(jnp.logical_and(here, k == r), lambda: share_j(k, k, (k, home)).wait_recv())
    both = got_i[0]
    for k in range(1, cols):
        both = both + got_i[k]
    for k in range(rows):
        both = both + got_j[k]
    o_left[...] = both[0]

    for k in range(rows):
        unless(k == r, lambda: two(k, k).wait_recv())
    acc = got2[0]
    for k in range(1, rows):
        acc = acc + got2[k]
    total[c, r] = acc
    for k in range(rows):
        unless(k == r, lambda: three(k, r).start())
    right_sum[...] = both[1]

    @pl.when(here)
    def _():
        o_right[slot] = both[1]

    for k in range(rows):
        unless(jnp.logical_and(here, k == r), lambda: spread(k, slot, (k, home)).start())
    for k in range(rows):
        unless(k == r, lambda: three(k, k).wait_recv())
    for k in range(cols):
        unless(k == c, lambda: four(k, c).start())
    for k in range(cols):
        unless(k == c, lambda: four(k, k).wait_recv())
    flat = total[...].reshape(-1, width) * (1.0 / residues)
    hidden_width = o_in.shape[1]
    for k in range(hidden_width // width):
        o_in[:, k * width : (k + 1) * width] = flat[k * width : (k + 1) * width]
    o_out[...] = flat[hidden_width : 2 * hidden_width]
    o_bins[...] = flat[2 * hidden_width : 2 * hidden_width + o_bins.shape[1]].T
    for k in range(rows):
        unless(jnp.logical_and(here, k == slot), lambda: spread(k, k, owner(k)).wait_recv())
    for k in range(cols):
        unless(k == c, lambda: one(k, c).wait_send())
        unless(k == c, lambda: share_i(k, c).wait_send())
        unless(k == c, lambda: four(k, c).wait_send())
    for k in range(rows):
        unless(k == r, lambda: two(k, r).wait_send())
        unless(k == r, lambda: three(k, r).wait_send())
        unless(jnp.logical_and(here, k == slot), lambda: share_j(k, r, owner(k)).wait_send())
        unless(jnp.logical_and(here, k == r), lambda: spread(k, slot, (k, home)).wait_send())


def on_device(plans, left_act, right_act, norm_gain, norm_bias, w_in, b_in, w_out, w_bins, labels):
    rows, cols = lax.axis_size("row"), lax.axis_size("col")
    chunk, width = left_act.shape
    hidden, bins = w_in.shape[1], w_bins.shape[1]
    residues = chunk * rows * cols
    vmem = pl.BlockSpec(memory_space=pltpu.VMEM)
    shape = jax.ShapeDtypeStruct
    dma = pltpu.SemaphoreType.DMA
    row_in, col_in = pl.pallas_call(
        functools.partial(gather_kernel, rows, cols),
        out_shape=(shape((cols, 2, chunk, width), BF16), shape((rows, 2, chunk, width), BF16)),
        in_specs=[vmem] * 2,
        out_specs=(vmem,) * 2,
        scratch_shapes=[dma((cols, 2)), dma((cols, 2)), dma((rows, 2)), dma((rows, 2))],
        compiler_params=pltpu.CompilerParams(collective_id=0, has_side_effects=True),
        name="gather",
    )(left_act, right_act)
    tab = lax.dynamic_index_in_dim(
        plans, lax.axis_index("row") * cols + lax.axis_index("col"), 0, keepdims=False
    )
    piece = -(-(2 * hidden + bins) // (rows * cols * SUB)) * SUB
    packed, res_i, res_j = pair_work(
        tab, row_in, col_in, norm_gain, norm_bias, w_in, b_in, w_out, w_bins, labels,
        rows * cols * piece,
    )
    packed = packed.reshape(cols, rows, piece, width)
    part = packed.shape[1:]
    grad_left, grad_right, grad_in, grad_out, grad_bins = pl.pallas_call(
        functools.partial(reduce_kernel, rows, cols, residues),
        out_shape=(
            shape((chunk, width), F32), shape((rows, chunk, width), F32),
            shape((width, hidden), F32), shape((hidden, width), F32), shape((width, bins), F32),
        ),
        in_specs=[vmem] * 3,
        out_specs=(vmem,) * 5,
        scratch_shapes=[
            pltpu.VMEM(packed.shape, F32), pltpu.VMEM(part, F32), pltpu.VMEM(part, F32),
            pltpu.VMEM(packed.shape, F32), pltpu.VMEM(res_i.shape, F32),
            pltpu.VMEM(res_j.shape, F32), pltpu.VMEM((chunk, width), F32),
            dma((cols,)), dma((cols,)), dma((rows,)), dma((rows,)), dma((rows,)), dma((rows,)),
            dma((cols,)), dma((cols,)), dma((cols,)), dma((cols,)), dma((rows,)), dma((rows,)),
            dma((rows,)), dma((rows,)),
        ],
        compiler_params=pltpu.CompilerParams(collective_id=1, has_side_effects=True),
        name="reduce",
    )(packed, res_i, res_j)
    return (grad_left, grad_right.reshape(-1, width), grad_in, grad_out, grad_bins)


def solution(mesh):
    placed = (
        P(("row", "col"), None),
        P(("row", "col"), None),
        P(),
        P(),
        P(),
        P(),
        P(),
        P(),
        P("row", "col"),
    )
    rows, cols = mesh.shape["row"], mesh.shape["col"]

    def step(*args):
        residues = args[8].shape[0]
        plans = jnp.asarray(schedule(rows, cols, residues // rows, residues // cols))
        return jax.shard_map(
            lambda *local: on_device(plans, *local),
            mesh=mesh,
            in_specs=placed,
            out_specs=(P(("row", "col"), None), P("col", None), P(), P(), P()),
            check_vma=False,
        )(*args)

    return step
```

```python
import functools

import jax
import jax.numpy as jnp
import numpy as np
from jax import lax
from jax.experimental import pallas as pl
from jax.experimental.pallas import tpu as pltpu
from jax.sharding import PartitionSpec as P

UNITS = 30
SUB = 8
F32 = jnp.float32
BF16 = jnp.bfloat16


def dims(first, second):
    return (((first,), (second,)), ((), ()))


def schedule(rows, cols, tile_rows, tile_cols):
    plans = []
    for r in range(rows):
        for c in range(cols):
            plan = []
            for i in range(tile_rows // SUB):
                for j in range(tile_cols // SUB):
                    big_i = r * tile_rows // SUB + i
                    big_j = c * tile_cols // SUB + j
                    if big_i == big_j:
                        plan.append((i, j, 1))
                    elif ((big_i + big_j) % 2 == 1) == (big_j > big_i):
                        plan.append((i, j, 2))
            plans.append(plan)
    longest = -(-max(map(len, plans)) // UNITS) * UNITS
    table = np.zeros((len(plans), 3, longest + 1), np.int32)
    for place, plan in enumerate(plans):
        table[place, :, : len(plan)] = np.array(plan, np.int32).T
        table[place, 0, longest] = -(-len(plan) // UNITS)
    return table


def pair_kernel(
    tab, row_in, col_in, gain_ref, bias_ref, w_in_ref, b_ref, w_out_ref, w_bins_ref, lab,
    packed, res_i, res_j,
    w_in_h, b_h, w_in_t, w_out_t_h, bins_t2, bins_t, raw_li, raw_ri, cen_li, cen_ri, raw_lj,
    raw_rj, cen_lj, cen_rj, acc_li, acc_ri, o_left_j, o_right_j, g_in, g_out, acc_bins,
):
    width = gain_ref.shape[1]
    scale = 1.0 / width
    half = UNITS * SUB * SUB
    last = tab.shape[1] - 1
    col_blocks = raw_lj.shape[0] // SUB

    chunk = row_in.shape[2]

    def whole(source, side):
        parts = [source[k, side].astype(F32) for k in range(source.shape[0])]
        return jnp.concatenate(parts, axis=0)

    for side, raw, cen in ((0, raw_li, cen_li), (1, raw_ri, cen_ri)):
        value = whole(row_in, side)
        mid = value - jnp.sum(value, axis=-1, keepdims=True) * scale
        raw[...] = jnp.broadcast_to(value[:, None, :], raw.shape)
        cen[...] = jnp.broadcast_to(mid[:, None, :], cen.shape)
    for side, raw, cen in ((0, raw_lj, cen_lj), (1, raw_rj, cen_rj)):
        value = whole(col_in, side)
        raw[...] = value
        cen[...] = value - jnp.sum(value, axis=-1, keepdims=True) * scale
    w_in = w_in_ref[...].astype(F32)
    w_in_h[...] = (w_in * 0.5).astype(BF16)
    w_in_t[...] = w_in.T.astype(BF16)
    b_h[...] = b_ref[...] * 0.5
    w_out_t_h[...] = (w_out_ref[...].astype(F32) * 0.5).T.astype(BF16)
    turned = w_bins_ref[...].astype(F32).T.astype(BF16)
    bins_t[...] = turned
    bins_t2[...] = jnp.concatenate([turned, turned], axis=1)
    for ref in (g_in, g_out, acc_bins, o_left_j, o_right_j, acc_li, acc_ri):
        ref[...] = jnp.zeros_like(ref)

    lane = lax.broadcasted_iota(jnp.int32, (1, 2 * SUB * SUB), 1)
    first_half = lane < SUB * SUB

    def step(s, carry):
        places = [(tab[0, s * UNITS + u], tab[1, s * UNITS + u]) for u in range(UNITS)]
        rows = [pl.ds(pl.multiple_of(i * SUB, SUB), SUB) for i, j in places]
        cols = [pl.ds(pl.multiple_of(j * SUB, SUB), SUB) for i, j in places]

        def grid(li, rj, ri, lj):
            own = [(li[a] + rj[b][None]).reshape(SUB * SUB, width) for a, b in zip(rows, cols)]
            far = [(ri[a] + lj[b][None]).reshape(SUB * SUB, width) for a, b in zip(rows, cols)]
            return jnp.concatenate(own + far, axis=0)

        center = grid(cen_li, cen_rj, cen_ri, cen_lj)
        inv = lax.rsqrt(jnp.sum(center * center, axis=-1, keepdims=True) * scale + 1e-05)
        form = center * inv
        normed = (form * gain_ref[...] + bias_ref[...]).astype(BF16)
        u = jnp.dot(normed, w_in_h[...], preferred_element_type=F32) + b_h[...]
        t = jnp.tanh(u)
        up = 1.0 + t
        act = u * up
        slope = up + act * (1.0 - t)
        hidden = act.astype(BF16)
        updated = (
            grid(raw_li, raw_rj, raw_ri, raw_lj)
            + jnp.dot(hidden, w_out_ref[...], preferred_element_type=F32)
        ).astype(BF16)
        both = jnp.concatenate([updated[:half], updated[half:]], axis=1)
        sym = lax.dot_general(bins_t2[...], both, dims(1, 1), preferred_element_type=F32)
        expo = jnp.exp(sym - jnp.max(sym, axis=0, keepdims=True))
        probs = expo / jnp.sum(expo, axis=0, keepdims=True)
        labs, scales = [], []
        for u0 in range(0, UNITS, 2):
            (ia, ja), (ib, jb) = places[u0], places[u0 + 1]
            labs.append(
                jnp.where(first_half, lab[ia * col_blocks + ja], lab[ib * col_blocks + jb])
            )
            wa = tab[2, s * UNITS + u0].astype(F32)
            wb = tab[2, s * UNITS + u0 + 1].astype(F32)
            scales.append(jnp.where(first_half, wa, wb))
        labs = jnp.concatenate(labs, axis=1)
        scales = jnp.concatenate(scales, axis=1)
        hit = lax.broadcasted_iota(jnp.int32, sym.shape, 0) == labs
        logit_grad = ((probs - jnp.where(hit, 1.0, 0.0)) * scales).astype(BF16)
        acc_bins[...] += jnp.dot(logit_grad, both, preferred_element_type=F32)
        upd_grad = lax.dot_general(
            logit_grad, bins_t[...], dims(0, 0), preferred_element_type=F32
        )
        upd_half = upd_grad.astype(BF16)
        hid_grad = jnp.dot(upd_half, w_out_t_h[...], preferred_element_type=F32)
        pre_grad = jnp.concatenate(
            [(hid_grad * slope[:half]).astype(BF16), (hid_grad * slope[half:]).astype(BF16)], axis=0
        )
        g_in[...] += lax.dot_general(normed, pre_grad, dims(0, 0), preferred_element_type=F32)
        g_out[...] += lax.dot_general(
            jnp.concatenate([upd_half, upd_half], axis=0), hidden, dims(0, 0),
            preferred_element_type=F32,
        )
        norm_grad = jnp.dot(pre_grad, w_in_t[...], preferred_element_type=F32) * gain_ref[...]
        mean = jnp.sum(norm_grad, axis=-1, keepdims=True) * scale
        mixed = jnp.sum(norm_grad * form, axis=-1, keepdims=True) * scale
        pair = inv * (norm_grad - mean - form * mixed)
        own = (pair[:half] + upd_grad).reshape(UNITS, SUB, SUB, width)
        far = (pair[half:] + upd_grad).reshape(UNITS, SUB, SUB, width)
        for k in range(UNITS):
            acc_li[rows[k]] += own[k]
            o_right_j[cols[k]] += jnp.sum(own[k], axis=0)
            acc_ri[rows[k]] += far[k]
            o_left_j[cols[k]] += jnp.sum(far[k], axis=0)
        return carry

    lax.fori_loop(0, tab[0, last], step, 0)
    for side, acc in ((0, acc_li), (1, acc_ri)):
        value = jnp.sum(acc[...], axis=1)
        for k in range(res_i.shape[0]):
            res_i[k, side] = value[k * chunk : (k + 1) * chunk]
    for side, acc in ((0, o_left_j), (1, o_right_j)):
        for k in range(res_j.shape[0]):
            res_j[k, side] = acc[k * chunk : (k + 1) * chunk]
    hidden_width = g_in.shape[1]
    for k in range(hidden_width // width):
        packed[k * width : (k + 1) * width] = g_in[:, k * width : (k + 1) * width]
    packed[hidden_width : 2 * hidden_width] = g_out[...].T
    end = 2 * hidden_width + acc_bins.shape[0]
    packed[2 * hidden_width : end] = acc_bins[:, :width] + acc_bins[:, width:]
    if end < packed.shape[0]:
        packed[end:] = jnp.zeros((packed.shape[0] - end, width), F32)


def pair_work(tab, row_in, col_in, gain, bias, w_in, b_in, w_out, w_bins, labels, packed_rows):
    tile_rows, tile_cols = labels.shape
    width, hidden = w_in.shape
    bins = w_bins.shape[1]
    blocks = labels.reshape(tile_rows // SUB, SUB, tile_cols // SUB, SUB)
    blocks = jnp.transpose(blocks, (0, 2, 1, 3)).reshape(-1, 1, SUB * SUB)
    lab = jnp.concatenate([blocks, blocks], axis=2)
    vmem = pl.BlockSpec(memory_space=pltpu.VMEM)
    shape = jax.ShapeDtypeStruct
    return pl.pallas_call(
        pair_kernel,
        out_shape=(
            shape((packed_rows, width), F32), shape(row_in.shape, F32), shape(col_in.shape, F32),
        ),
        in_specs=[pl.BlockSpec(memory_space=pltpu.SMEM)] + [vmem] * 9,
        out_specs=(vmem,) * 3,
        scratch_shapes=[
            pltpu.VMEM((width, hidden), BF16), pltpu.VMEM((1, hidden), F32),
            pltpu.VMEM((hidden, width), BF16), pltpu.VMEM((width, hidden), BF16),
            pltpu.VMEM((bins, 2 * width), BF16), pltpu.VMEM((bins, width), BF16),
        ]
        + [pltpu.VMEM((tile_rows, SUB, width), F32)] * 4
        + [pltpu.VMEM((tile_cols, width), F32)] * 4
        + [pltpu.VMEM((tile_rows, SUB, width), F32)] * 2
        + [pltpu.VMEM((tile_cols, width), F32)] * 2
        + [pltpu.VMEM((width, hidden), F32)] * 2
        + [pltpu.VMEM((bins, 2 * width), F32)],
        compiler_params=pltpu.CompilerParams(),
        name="pairs",
    )(tab, row_in, col_in, gain[None], bias[None], w_in, b_in[None], w_out, w_bins, lab)


def partners(rows, cols):
    r, c = lax.axis_index("row"), lax.axis_index("col")
    place = r * cols + c
    home = place // rows
    slot = place % rows

    def owner(m):
        k = c * rows + m
        return (k // cols, k % cols)

    return r, c, home, slot, owner


def unless(skip, action):
    if skip is None:
        action()
    else:
        pl.when(jnp.logical_not(skip))(action)


def greet(rows, cols, with_column):
    r, c, home, slot, owner = partners(rows, cols)
    barrier = pltpu.get_barrier_semaphore()

    def hello(device, skip):
        unless(skip, lambda: pl.semaphore_signal(
            barrier, inc=1, device_id=device, device_id_type=pl.DeviceIdType.MESH))

    for k in range(cols):
        hello((r, k), k == c)
    for k in range(rows):
        if with_column:
            hello((k, c), k == r)
        hello((k, home), jnp.logical_and(k == r, home == c))
        hello(owner(k), jnp.logical_and(home == c, k == slot))
    count = cols - 1 + 2 * rows + (rows - 1 if with_column else 0)
    pl.semaphore_wait(barrier, count - 2 * jnp.where(home == c, 1, 0))


def remote(src, dst, send, recv, device):
    return pltpu.make_async_remote_copy(
        src_ref=src, dst_ref=dst, send_sem=send, recv_sem=recv, device_id=device,
        device_id_type=pl.DeviceIdType.MESH,
    )


def gather_kernel(rows, cols, left, right, row_out, col_out, s_row, r_row, s_col, r_col):
    r, c, home, slot, owner = partners(rows, cols)
    here = home == c
    greet(rows, cols, False)
    sides = ((0, left), (1, right))

    def row_copy(side, src, k, at):
        return remote(src, row_out.at[at, side], s_row.at[k, side], r_row.at[at, side], (r, k))

    def col_copy(side, src, k, at, device):
        return remote(src, col_out.at[at, side], s_col.at[k, side], r_col.at[at, side], device)

    for side, src in sides:
        for k in range(rows):
            unless(jnp.logical_and(here, k == r),
                   lambda: col_copy(side, src, k, slot, (k, home)).start())
        for k in range(cols):
            unless(k == c, lambda: row_copy(side, src, k, c).start())
    for side, src in sides:
        row_out[c, side] = src[...]

        @pl.when(here)
        def _():
            col_out[slot, side] = src[...]

    for side, src in sides:
        for k in range(cols):
            unless(k == c, lambda: row_copy(side, src, k, k).wait_recv())
        for k in range(rows):
            unless(jnp.logical_and(here, k == slot),
                   lambda: col_copy(side, src, k, k, owner(k)).wait_recv())
    for side, src in sides:
        for k in range(cols):
            unless(k == c, lambda: row_copy(side, src, k, c).wait_send())
        for k in range(rows):
            unless(jnp.logical_and(here, k == r),
                   lambda: col_copy(side, src, k, slot, (k, home)).wait_send())


def reduce_kernel(
    rows, cols, mine, res_i, res_j, total, o_left, o_right,
    got1, sum1, got2, got_i, got_j, right_sum,
    s1, r1, s2, r2, s3, r3, s4, r4, si, ri, sj, rj, sb, rb,
):
    r, c, home, slot, owner = partners(rows, cols)
    here = home == c
    greet(rows, cols, True)
    order = [lax.rem(r + 1 + i, rows) for i in range(rows)]

    def one(k, i, at):
        return remote(
            mine.at[k, order[i]], got1.at[at, i], s1.at[k, i], r1.at[at, i], (r, k)
        )

    def two(i):
        return remote(sum1.at[i], got2.at[r], s2.at[i], r2.at[r], (order[i], c))

    def two_in(i):
        return remote(sum1.at[i], got2.at[order[i]], s2.at[i], r2.at[order[i]], (order[i], c))

    def three(i, at):
        return remote(total.at[c, r], total.at[c, at], s3.at[i], r3.at[at], (order[i], c))

    def four(k, i, at):
        return remote(
            total.at[c, order[i]], total.at[at, order[i]], s4.at[k, i], r4.at[at, i], (r, k)
        )

    def share_i(k, at):
        return remote(res_i.at[k], got_i.at[at], si.at[k], ri.at[at], (r, k))

    def share_j(k, at, device):
        return remote(res_j.at[k], got_j.at[at], sj.at[k], rj.at[at], device)

    def spread(k, at, device):
        return remote(right_sum, o_right.at[at], sb.at[k], rb.at[at], device)

    for k in range(rows):
        unless(jnp.logical_and(here, k == slot), lambda: share_j(k, r, owner(k)).start())
    for i in range(rows):
        for k in range(cols):
            unless(k == c, lambda: one(k, i, c).start())
    for k in range(cols):
        unless(k == c, lambda: share_i(k, c).start())
    got_i[c] = res_i[c]

    @pl.when(here)
    def _():
        got_j[r] = res_j[slot]

    for i in range(rows):
        got1[c, i] = mine[c, order[i]]
    for i in range(rows):
        for k in range(cols):
            unless(k == c, lambda: one(k, i, k).wait_recv())
        acc = got1[0, i]
        for k in range(1, cols):
            acc = acc + got1[k, i]
        sum1[i] = acc
        if i < rows - 1:
            two(i).start()
    got2[r] = sum1[rows - 1]

    for k in range(cols):
        unless(k == c, lambda: share_i(k, k).wait_recv())
    for k in range(rows):
        unless(jnp.logical_and(here, k == r), lambda: share_j(k, k, (k, home)).wait_recv())
    both = got_i[0]
    for k in range(1, cols):
        both = both + got_i[k]
    for k in range(rows):
        both = both + got_j[k]
    o_left[...] = both[0]
    right_sum[...] = both[1]

    @pl.when(here)
    def _():
        o_right[slot] = both[1]

    for i in range(rows - 1):
        two_in(i).wait_recv()
    acc = got2[0]
    for k in range(1, rows):
        acc = acc + got2[k]
    total[c, r] = acc
    for i in range(rows - 1):
        three(i, r).start()
    for k in range(cols):
        unless(k == c, lambda: four(k, rows - 1, c).start())
    for k in range(rows):
        unless(jnp.logical_and(here, k == r), lambda: spread(k, slot, (k, home)).start())
    for i in range(rows - 1):
        three(i, order[i]).wait_recv()
        for k in range(cols):
            unless(k == c, lambda: four(k, i, c).start())
    for i in range(rows):
        for k in range(cols):
            unless(k == c, lambda: four(k, i, k).wait_recv())
    for k in range(rows):
        unless(jnp.logical_and(here, k == slot), lambda: spread(k, k, owner(k)).wait_recv())
    for k in range(cols):
        for i in range(rows):
            unless(k == c, lambda: one(k, i, c).wait_send())
            unless(k == c, lambda: four(k, i, c).wait_send())
        unless(k == c, lambda: share_i(k, c).wait_send())
    for i in range(rows - 1):
        two(i).wait_send()
        three(i, r).wait_send()
    for k in range(rows):
        unless(jnp.logical_and(here, k == slot), lambda: share_j(k, r, owner(k)).wait_send())
        unless(jnp.logical_and(here, k == r), lambda: spread(k, slot, (k, home)).wait_send())


def finish_kernel(residues, total, left, right, o_left, o_right, o_in, o_out, o_bins):
    width, hidden_width = o_in.shape
    flat = total[...].reshape(-1, width) * (1.0 / residues)
    for k in range(hidden_width // width):
        o_in[:, k * width : (k + 1) * width] = flat[k * width : (k + 1) * width]
    o_out[...] = flat[hidden_width : 2 * hidden_width]
    o_bins[...] = flat[2 * hidden_width : 2 * hidden_width + o_bins.shape[1]].T
    o_left[...] = left[...]
    o_right[...] = right[...]


def on_device(plans, left_act, right_act, norm_gain, norm_bias, w_in, b_in, w_out, w_bins, labels):
    rows, cols = lax.axis_size("row"), lax.axis_size("col")
    chunk, width = left_act.shape
    hidden, bins = w_in.shape[1], w_bins.shape[1]
    residues = chunk * rows * cols
    vmem = pl.BlockSpec(memory_space=pltpu.VMEM)
    shape = jax.ShapeDtypeStruct
    dma = pltpu.SemaphoreType.DMA
    row_in, col_in = pl.pallas_call(
        functools.partial(gather_kernel, rows, cols),
        out_shape=(shape((cols, 2, chunk, width), BF16), shape((rows, 2, chunk, width), BF16)),
        in_specs=[vmem] * 2,
        out_specs=(vmem,) * 2,
        scratch_shapes=[dma((cols, 2)), dma((cols, 2)), dma((rows, 2)), dma((rows, 2))],
        compiler_params=pltpu.CompilerParams(collective_id=0, has_side_effects=True),
        name="gather",
    )(left_act, right_act)
    tab = lax.dynamic_index_in_dim(
        plans, lax.axis_index("row") * cols + lax.axis_index("col"), 0, keepdims=False
    )
    piece = -(-(2 * hidden + bins) // (rows * cols * SUB)) * SUB
    packed, res_i, res_j = pair_work(
        tab, row_in, col_in, norm_gain, norm_bias, w_in, b_in, w_out, w_bins, labels,
        rows * cols * piece,
    )
    packed = packed.reshape(cols, rows, piece, width)
    part = packed.shape[1:]
    grid = (cols, rows)
    total, left_sum, right_sum = pl.pallas_call(
        functools.partial(reduce_kernel, rows, cols),
        out_shape=(
            shape(packed.shape, F32), shape((chunk, width), F32), shape((rows, chunk, width), F32),
        ),
        in_specs=[vmem] * 3,
        out_specs=(vmem,) * 3,
        scratch_shapes=[
            pltpu.VMEM(packed.shape, F32), pltpu.VMEM(part, F32), pltpu.VMEM(part, F32),
            pltpu.VMEM(res_i.shape, F32), pltpu.VMEM(res_j.shape, F32),
            pltpu.VMEM((chunk, width), F32),
            dma(grid), dma(grid), dma((rows,)), dma((rows,)), dma((rows,)), dma((rows,)),
            dma(grid), dma(grid), dma((cols,)), dma((cols,)), dma((rows,)), dma((rows,)),
            dma((rows,)), dma((rows,)),
        ],
        compiler_params=pltpu.CompilerParams(collective_id=1, has_side_effects=True),
        name="reduce",
    )(packed, res_i, res_j)
    grad_left, grad_right, grad_in, grad_out, grad_bins = pl.pallas_call(
        functools.partial(finish_kernel, residues),
        out_shape=(
            shape((chunk, width), F32), shape((rows, chunk, width), F32),
            shape((width, hidden), F32), shape((hidden, width), F32), shape((width, bins), F32),
        ),
        in_specs=[vmem] * 3,
        out_specs=(vmem,) * 5,
        name="finish",
    )(total, left_sum, right_sum)
    return (grad_left, grad_right.reshape(-1, width), grad_in, grad_out, grad_bins)


def solution(mesh):
    placed = (
        P(("row", "col"), None),
        P(("row", "col"), None),
        P(),
        P(),
        P(),
        P(),
        P(),
        P(),
        P("row", "col"),
    )
    rows, cols = mesh.shape["row"], mesh.shape["col"]

    def step(*args):
        residues = args[8].shape[0]
        plans = jnp.asarray(schedule(rows, cols, residues // rows, residues // cols))
        return jax.shard_map(
            lambda *local: on_device(plans, *local),
            mesh=mesh,
            in_specs=placed,
            out_specs=(P(("row", "col"), None), P("col", None), P(), P(), P()),
            check_vma=False,
        )(*args)

    return step
```
